32 devices in a mesh: freq: 4 (over z), row: 4 (over y, x), col: 2 (over core).
Axes of the slice: x: 2, y: 2, z: 4, core: 2. Of those that a mesh axis runs over, the one named last changes fastest.
Arguments:
- prior_factor: bfloat16 [4, 26624, 1024], P('freq', ('row', 'col')), may hold values from -1 to 1, as said below
- prior_seeds: int32 [4, 26624, 512], P('freq', ('row', 'col')), may hold values from 0 to 4095
- window_seeds: int32 [4, 1024, 512], P('freq'), may hold values from 0 to 4095
- spectra: float32 [4, 1024], P('freq'), may hold values from 0.25 to 1
- nugget: float32 [4, 1024], P('freq'), may hold values from 0.6 to 1.2
- decay: float32 [4], P('freq'), may hold values from 0.2 to 2
Outputs:
- velocity: float32 [512, 1024, 256], P('freq', ('row', 'col'))
The draws below stay inside these ranges and needn't reach their ends.
Inputs may be any that keep to these rules, and one draw needn't show every extreme that they name: `prior_factor`: every entry is smaller in magnitude than 0.95 / (sqrt(26624) + sqrt(1024)), and window_matrix is positive definite.
All inputs are finite; a program needn't handle non-finite values.
Results may differ from the reference program's by a relative error of at most 0.00087.
Values sent between devices are 32-bit elements; how exact they have to be, the bound alone decides.
A program may use at most 128 MiB of HBM per device.

```python
import math
import jax
import jax.numpy as jnp
from jax import lax

GRID = 96
NPHASE = 4096
SEEDS = 512
STEPS = 256
WINDOW = 1024
PRIOR = 26624
FREQS = 4
FIRST_BIN = 64
N_ROW = 4
N_COL = 2


def draw_prior_factor(key, part):
    limit = math.sqrt(0.9) / (math.sqrt(PRIOR) + math.sqrt(WINDOW))
    values = jax.random.uniform(key, (FREQS, PRIOR, WINDOW), jnp.float32, -limit, limit)
    return values.astype(jnp.bfloat16)


def plant(result, stream_key, smallest, high):
    dims = result.shape
    spot = [jax.random.randint(jax.random.fold_in(stream_key, axis), (), 0, dims[axis]) for axis in range(len(dims))]
    result = result.at[tuple(spot)].set(smallest)
    longest = dims.index(max(dims))
    spot[longest] = (spot[longest] + 1) % dims[longest]
    return result.at[tuple(spot)].set(high)


def steps_of(rng, dims, split, least, high):
    def one(axis_at, blocks):
        steps = jax.random.uniform(jax.random.fold_in(jax.random.fold_in(rng, 6), axis_at), (blocks,), jnp.float32, least / len(split), high / len(split))
        return jnp.repeat(jnp.exp(steps), dims[axis_at] // blocks).reshape((-1,) + (1,) * (len(dims) - axis_at - 1))

    gain = one(*split[0])
    for cut in split[1:]:
        gain = gain * one(*cut)
    return gain


def setup_inputs(seed: int = 0) -> dict:
    arg_keys = jax.random.split(jax.random.key(seed), 7)
    return {
        "prior_factor": draw_prior_factor(jax.random.fold_in(arg_keys[6], 71), 0),
        "prior_seeds": plant(jax.random.randint(arg_keys[1], (FREQS, PRIOR, SEEDS), 0, NPHASE), jax.random.fold_in(arg_keys[1], 1), 0, NPHASE - 1).astype(jnp.int32),
        "window_seeds": plant(jax.random.randint(arg_keys[2], (FREQS, WINDOW, SEEDS), 0, NPHASE), jax.random.fold_in(arg_keys[2], 1), 0, NPHASE - 1).astype(jnp.int32),
        "spectra": jnp.clip(jnp.exp(math.log(1.0) - 1.3862944 * jax.random.uniform(arg_keys[3], (FREQS, WINDOW), jnp.float32) ** steps_of(arg_keys[3], (FREQS, WINDOW), ((0, 4),), -0.2, 0.2)), 0.25, 1.0),
        "nugget": jnp.clip(0.6 + 0.6 * jax.random.uniform(arg_keys[4], (FREQS, WINDOW), jnp.float32) ** steps_of(arg_keys[4], (FREQS, WINDOW), ((0, 4),), -0.2, 0.2), 0.6, 1.2),
        "decay": jnp.clip(jnp.exp(math.log(2.0) - 2.3025851 * jax.random.uniform(arg_keys[5], (FREQS,), jnp.float32) ** steps_of(arg_keys[5], (FREQS,), ((0, 4),), -0.2, 0.2)), 0.2, 2.0),
    }


cross_weight = 0.3

def window_index(positions, window, parts):
    own = window // parts
    quarter = own // 2
    device = positions // own
    within = positions % own
    return jnp.where(within < quarter, device * quarter + within, window // 2 + device * quarter + within - quarter).astype(jnp.int32)

def coherence(spectra, nugget, decay, row_ids):
    window = spectra.shape[0]
    col_ids = jnp.arange(window, dtype=jnp.int32)
    row_global = PRIOR + row_ids
    col_global = PRIOR + col_ids
    row_points = row_global // 3
    col_points = col_global // 3
    row_across = (row_points % GRID).astype(jnp.float32)
    row_height = (row_points // GRID).astype(jnp.float32)
    col_across = (col_points % GRID).astype(jnp.float32)
    col_height = (col_points // GRID).astype(jnp.float32)
    distance = jnp.sqrt((row_across[:, None] - col_across[None, :]) ** 2 + (row_height[:, None] - col_height[None, :]) ** 2)
    coupling = jnp.where((row_global % 3)[:, None] == (col_global % 3)[None, :], jnp.float32(1.0), jnp.float32(cross_weight))
    row_spectra = jnp.take(spectra, row_ids)
    row_nugget = jnp.take(nugget, row_ids)
    amplitude = jnp.sqrt(row_spectra[:, None] * spectra[None, :])
    diagonal = jnp.where(row_ids[:, None] == col_ids[None, :], row_nugget[:, None], jnp.float32(0.0))
    return coupling * amplitude * jnp.exp(-decay * distance) + diagonal

def reference(prior_factor, prior_seeds, window_seeds, spectra, nugget, decay):
    re_parts = []
    im_parts = []
    natural_ids = jnp.arange(WINDOW, dtype=jnp.int32)
    for freq_index in range(FREQS):
        prior_cols = prior_factor[freq_index]
        schur = jnp.dot(prior_cols.T.astype(jnp.float32), prior_cols.astype(jnp.float32), preferred_element_type=jnp.float32)
        window_matrix = coherence(spectra[freq_index], nugget[freq_index], decay[freq_index], natural_ids) - schur
        factor = jnp.linalg.cholesky(window_matrix)
        phases = 2.0 * math.pi / NPHASE * prior_seeds[freq_index].astype(jnp.float32)
        wave_re = jnp.cos(phases).astype(jnp.bfloat16)
        wave_im = jnp.sin(phases).astype(jnp.bfloat16)
        prior_re = jnp.dot(prior_cols.T.astype(jnp.float32), wave_re.astype(jnp.float32), preferred_element_type=jnp.float32)
        prior_im = jnp.dot(prior_cols.T.astype(jnp.float32), wave_im.astype(jnp.float32), preferred_element_type=jnp.float32)
        window_phases = 2.0 * math.pi / NPHASE * window_seeds[freq_index].astype(jnp.float32)
        re_parts.append(prior_re + jnp.dot(factor, jnp.cos(window_phases), precision=lax.Precision.HIGHEST))
        im_parts.append(prior_im + jnp.dot(factor, jnp.sin(window_phases), precision=lax.Precision.HIGHEST))
    amp_re = jnp.stack(re_parts)
    amp_im = jnp.stack(im_parts)
    freq_bins = FIRST_BIN + jnp.arange(FREQS, dtype=jnp.int32)
    sample_ids = jnp.arange(STEPS, dtype=jnp.int32)
    turns = (freq_bins[:, None] * sample_ids[None, :] % STEPS).astype(jnp.float32) * (2.0 * math.pi / STEPS)
    first_sum = jnp.einsum('fps,ft->spt', amp_re, jnp.cos(turns), precision=lax.Precision.HIGHEST)
    second_sum = jnp.einsum('fps,ft->spt', amp_im, jnp.sin(turns), precision=lax.Precision.HIGHEST)
    natural = first_sum - second_sum
    stored = window_index(natural_ids, WINDOW, N_ROW * N_COL)
    return jnp.take(natural, stored, axis=1)
```

```python
import functools
import math

import jax
import jax.numpy as jnp
from jax import lax
from jax.experimental import pallas as pl
from jax.experimental.pallas import tpu as pltpu
from jax.sharding import PartitionSpec as P

GRID = 96
NPHASE = 4096
STEPS = 256
PRIOR = 26624
FIRST_BIN = 64
AXES = ("row", "col")
BLOCK = 128
SUB = 8


def split(x):
    high = x.astype(jnp.bfloat16)
    return high, (x - high.astype(jnp.float32)).astype(jnp.bfloat16)


def mul_nt(a, b):
    dims = (((1,), (1,)), ((), ()))
    dot = functools.partial(lax.dot_general, dimension_numbers=dims, preferred_element_type=jnp.float32)
    ah, al = a
    bh, bl = b
    return dot(ah, bh) + (dot(ah, bl) + dot(al, bh))


def factor_block(m_ref, l_ref, col_ref, row_ref):
    lane = lax.broadcasted_iota(jnp.int32, (SUB, BLOCK), 1)
    sub = lax.broadcasted_iota(jnp.int32, (SUB, BLOCK), 0)
    strips = BLOCK // SUB
    for p in range(strips):
        j0 = SUB * p
        inside = (lane >= j0) & (lane < j0 + SUB)
        lead = m_ref[j0:j0 + SUB, :]
        for k in range(SUB):
            col_ref[k] = jnp.broadcast_to(lead[:, j0 + k:j0 + k + 1], (SUB, BLOCK))
        row_ref[...] = jnp.where(inside, jnp.where(lane - j0 == sub, 1.0, 0.0), lead)
        a = {}
        for k in range(SUB):
            for i in range(k, SUB):
                a[i, k] = jnp.broadcast_to(col_ref[k, i:i + 1, :], (SUB, BLOCK))
        inv = []
        low = {}
        for k in range(SUB):
            r = lax.rsqrt(a[k, k])
            inv.append(r)
            for i in range(k + 1, SUB):
                low[i, k] = a[i, k] * r
            for m in range(k + 1, SUB):
                for i in range(m, SUB):
                    a[i, m] = a[i, m] - low[i, k] * low[m, k]
        u = []
        for k in range(SUB):
            x = jnp.broadcast_to(row_ref[k:k + 1, :], (SUB, BLOCK))
            for m in range(k):
                x = x - low[k, m] * u[m]
            u.append(x * inv[k])
        w = u[0]
        for k in range(1, SUB):
            w = jnp.where(sub == k, u[k], w)
        m_ref[j0:j0 + SUB, :] = jnp.where(lane < j0 + SUB, w, 0.0)
        for t in range(p, strips):
            at = slice(SUB * t, SUB * t + SUB)
            rows = lead if t == p else m_ref[at, :]
            c = []
            lacc = l_ref[at, :]
            for k in range(SUB):
                x = jnp.broadcast_to(rows[:, j0 + k:j0 + k + 1], (SUB, BLOCK))
                for m in range(k):
                    x = x - low[k, m] * c[m]
                c.append(x * inv[k])
                here = lane == j0 + k
                if t == p:
                    here = here & (sub >= k)
                lacc = jnp.where(here, c[k], lacc)
            l_ref[at, :] = lacc
            if t > p:
                x = jnp.where(inside, 0.0, rows)
                for k in range(SUB):
                    x = x - c[k] * u[k]
                m_ref[at, :] = x


def chol_kernel(coh_ref, sum_ref, out_ref, m_ref, l_ref, col_ref, row_ref, pan_ref):
    window = out_ref.shape[0]
    wide = sum_ref.shape[1]
    out_ref[...] = jnp.zeros_like(out_ref)
    at = 0
    for j in range(window // wide):
        size = window - j * wide
        out_ref[j * wide:, j * wide:(j + 1) * wide] = (
            coh_ref[j * wide:, j * wide:(j + 1) * wide] - sum_ref[at:at + size, :]
        )
        at += size

    row = lax.broadcasted_iota(jnp.int32, (window, BLOCK), 0)

    @pl.loop(0, window // BLOCK)
    def _(b):
        here = pl.ds(pl.multiple_of(b * BLOCK, BLOCK), BLOCK)
        pan_ref[...] = out_ref[:, here]

        @pl.loop(0, b)
        def _(k):
            there = pl.ds(pl.multiple_of(k * BLOCK, BLOCK), BLOCK)
            pan_ref[...] -= mul_nt(split(out_ref[:, there]), split(out_ref[here, there]))

        m_ref[...] = pan_ref[here, :]
        l_ref[...] = jnp.zeros_like(l_ref)
        factor_block(m_ref, l_ref, col_ref, row_ref)
        below = mul_nt(split(pan_ref[...]), split(m_ref[...]))
        out_ref[:, here] = jnp.where(row >= (b + 1) * BLOCK, below, 0.0)
        out_ref[here, here] = l_ref[...]


def cholesky(coh, packed):
    window = coh.shape[0]
    return pl.pallas_call(
        chol_kernel,
        name="factor",
        out_shape=jax.ShapeDtypeStruct((window, window), jnp.float32),
        in_specs=[pl.BlockSpec(memory_space=pltpu.VMEM)] * 2,
        out_specs=pl.BlockSpec(memory_space=pltpu.VMEM),
        scratch_shapes=[
            pltpu.VMEM((BLOCK, BLOCK), jnp.float32),
            pltpu.VMEM((BLOCK, BLOCK), jnp.float32),
            pltpu.VMEM((SUB, SUB, BLOCK), jnp.float32),
            pltpu.VMEM((SUB, BLOCK), jnp.float32),
            pltpu.VMEM((window, BLOCK), jnp.float32),
        ],
        compiler_params=pltpu.CompilerParams(vmem_limit_bytes=40 * 2**20),
        cost_estimate=pl.CostEstimate(flops=40 * 10**9, bytes_accessed=11 * 2**20, transcendentals=0),
    )(coh, packed)


cross_weight = 0.3


def coherence(spectra, nugget, decay, row_ids):
    window = spectra.shape[0]
    col_ids = jnp.arange(window, dtype=jnp.int32)
    row_global = PRIOR + row_ids
    col_global = PRIOR + col_ids
    row_points = row_global // 3
    col_points = col_global // 3
    row_across = (row_points % GRID).astype(jnp.float32)
    row_height = (row_points // GRID).astype(jnp.float32)
    col_across = (col_points % GRID).astype(jnp.float32)
    col_height = (col_points // GRID).astype(jnp.float32)
    distance = jnp.sqrt(
        (row_across[:, None] - col_across[None, :]) ** 2
        + (row_height[:, None] - col_height[None, :]) ** 2
    )
    coupling = jnp.where(
        (row_global % 3)[:, None] == (col_global % 3)[None, :],
        jnp.float32(1.0),
        jnp.float32(cross_weight),
    )
    row_spectra = jnp.take(spectra, row_ids)
    row_nugget = jnp.take(nugget, row_ids)
    amplitude = jnp.sqrt(row_spectra[:, None] * spectra[None, :])
    diagonal = jnp.where(
        row_ids[:, None] == col_ids[None, :], row_nugget[:, None], jnp.float32(0.0)
    )
    return coupling * amplitude * jnp.exp(-decay * distance) + diagonal


def against(picked, other):
    return lax.dot_general(
        picked, other, (((0,), (0,)), ((), ())), preferred_element_type=jnp.float32
    )


def waves_of(seeds):
    quarter = NPHASE // 4
    turn = (seeds + quarter // 2) // quarter
    x = (seeds - turn * quarter).astype(jnp.float32) * (2.0 * math.pi / NPHASE)
    y = x * x
    sin = x * (1.0 + y * (-1 / 6 + y * (1 / 120 + y * (-1 / 5040 + y * (1 / 362880)))))
    cos = 1.0 + y * (-1 / 2 + y * (1 / 24 + y * (-1 / 720 + y * (1 / 40320))))
    odd = (turn & 1) == 1
    re = jnp.where(odd, sin, cos)
    im = jnp.where(odd, cos, sin)
    return (
        jnp.where(((turn + 1) & 2) == 2, -re, re),
        jnp.where((turn & 2) == 2, -im, im),
    )


def synth_kernel(x_ref, table_ref, out_ref):
    def parts(value):
        high = value.astype(jnp.bfloat16).astype(jnp.float32)
        return high, value - high

    xh, xl = parts(x_ref[...])
    th, tl = parts(table_ref[...])
    lhs = jnp.concatenate([xh, xh, xl, xl], axis=0).astype(jnp.bfloat16)
    rhs = jnp.concatenate([th, tl, th, tl], axis=0).astype(jnp.bfloat16)
    out_ref[...] = lax.dot_general(
        lhs, rhs, (((0,), (0,)), ((), ())), preferred_element_type=jnp.float32
    )


def synthesize(stacked, freq_count):
    freq_bins = FIRST_BIN + jnp.arange(freq_count, dtype=jnp.int32)
    sample_ids = jnp.arange(STEPS, dtype=jnp.int32)
    turns = (freq_bins[:, None] * sample_ids[None, :] % STEPS).astype(jnp.float32) * (
        2.0 * math.pi / STEPS
    )
    tables = jnp.stack([jnp.cos(turns), -jnp.sin(turns)], axis=1).reshape(2 * freq_count, STEPS)
    count = stacked.shape[1]
    step = min(2048, count)
    return pl.pallas_call(
        synth_kernel,
        name="synth",
        grid=(count // step,),
        out_shape=jax.ShapeDtypeStruct((count, STEPS), jnp.float32),
        in_specs=[
            pl.BlockSpec((2 * freq_count, step), lambda i: (0, i)),
            pl.BlockSpec((2 * freq_count, STEPS), lambda i: (0, 0)),
        ],
        out_specs=pl.BlockSpec((step, STEPS), lambda i: (i, 0)),
        compiler_params=pltpu.CompilerParams(vmem_limit_bytes=24 * 2**20),
    )(stacked, tables)


def shards(prior_factor, prior_seeds, window_seeds, spectra, nugget, decay):
    cols = prior_factor[0]
    window = cols.shape[1]
    parts = lax.axis_size(AXES)
    freq_count = lax.axis_size("freq")
    quarter = window // (2 * parts)
    seed_count = prior_seeds.shape[2]
    me = lax.axis_index(AXES)
    wide = 2 * BLOCK

    packed = jnp.concatenate(
        [against(cols[:, at:], cols[:, at:at + wide]) for at in range(0, window, wide)], axis=0
    )
    packed = lax.psum_scatter(packed, AXES, scatter_dimension=0, tiled=True)
    packed = lax.all_gather(packed, AXES, axis=0, tiled=True)

    def scattered(wave):
        whole = against(cols, wave.astype(jnp.bfloat16)).reshape(2, parts, quarter, seed_count)
        whole = jnp.transpose(whole, (1, 0, 2, 3)).reshape(window, seed_count)
        return lax.psum_scatter(whole, AXES, scatter_dimension=0, tiled=True)

    wave_re, wave_im = waves_of(prior_seeds[0])
    prior = jnp.concatenate([scattered(wave_re), scattered(wave_im)], axis=1)
    window_waves = jnp.concatenate(waves_of(window_seeds[0]), axis=1)

    coh = coherence(spectra[0], nugget[0], decay[0], jnp.arange(window, dtype=jnp.int32))
    factor = cholesky(coh, packed)
    own = jnp.concatenate(
        [
            lax.dynamic_slice_in_dim(factor, me * quarter, quarter, 0),
            lax.dynamic_slice_in_dim(factor, window // 2 + me * quarter, quarter, 0),
        ],
        axis=0,
    )
    amplitude = prior + jnp.dot(own, window_waves, precision=lax.Precision.HIGH)
    turned = amplitude.T.reshape(2, seed_count, 2 * quarter)
    spread = lax.all_to_all(turned, "freq", split_axis=1, concat_axis=0, tiled=True)
    here = seed_count // freq_count
    out = synthesize(spread.reshape(2 * freq_count, here * 2 * quarter), freq_count)
    return out.reshape(here, 2 * quarter, STEPS)


def solution(mesh):
    in_specs = (
        P("freq", ("row", "col"), None),
        P("freq", ("row", "col"), None),
        P("freq", None, None),
        P("freq", None),
        P("freq", None),
        P("freq"),
    )
    out_specs = P("freq", ("row", "col"), None)
    return jax.shard_map(shards, mesh=mesh, in_specs=in_specs, out_specs=out_specs, check_vma=False)
```

```python
import functools
import math

import jax
import jax.numpy as jnp
from jax import lax
from jax.experimental import pallas as pl
from jax.experimental.pallas import tpu as pltpu
from jax.sharding import PartitionSpec as P

GRID = 96
NPHASE = 4096
STEPS = 256
PRIOR = 26624
FIRST_BIN = 64
AXES = ("row", "col")
BLOCK = 128
SUB = 8


def split(x):
    high = x.astype(jnp.bfloat16)
    return high, (x - high.astype(jnp.float32)).astype(jnp.bfloat16)


def mul_nt(a, b):
    dims = (((1,), (1,)), ((), ()))
    dot = functools.partial(lax.dot_general, dimension_numbers=dims, preferred_element_type=jnp.float32)
    ah, al = a
    bh, bl = b
    return dot(ah, bh) + (dot(ah, bl) + dot(al, bh))


def factor_block(m_ref, l_ref, col_ref, row_ref):
    lane = lax.broadcasted_iota(jnp.int32, (SUB, BLOCK), 1)
    sub = lax.broadcasted_iota(jnp.int32, (SUB, BLOCK), 0)
    strips = BLOCK // SUB
    for p in range(strips):
        j0 = SUB * p
        inside = (lane >= j0) & (lane < j0 + SUB)
        lead = m_ref[j0:j0 + SUB, :]
        for k in range(SUB):
            col_ref[k] = jnp.broadcast_to(lead[:, j0 + k:j0 + k + 1], (SUB, BLOCK))
        row_ref[...] = jnp.where(inside, jnp.where(lane - j0 == sub, 1.0, 0.0), lead)
        a = {}
        for k in range(SUB):
            for i in range(k, SUB):
                a[i, k] = jnp.broadcast_to(col_ref[k, i:i + 1, :], (SUB, BLOCK))
        inv = []
        low = {}
        for k in range(SUB):
            r = lax.rsqrt(a[k, k])
            inv.append(r)
            for i in range(k + 1, SUB):
                low[i, k] = a[i, k] * r
            for m in range(k + 1, SUB):
                for i in range(m, SUB):
                    a[i, m] = a[i, m] - low[i, k] * low[m, k]
        u = []
        for k in range(SUB):
            x = jnp.broadcast_to(row_ref[k:k + 1, :], (SUB, BLOCK))
            for m in range(k):
                x = x - low[k, m] * u[m]
            u.append(x * inv[k])
        w = u[0]
        for k in range(1, SUB):
            w = jnp.where(sub == k, u[k], w)
        m_ref[j0:j0 + SUB, :] = jnp.where(lane < j0 + SUB, w, 0.0)
        for t in range(p, strips):
            at = slice(SUB * t, SUB * t + SUB)
            rows = lead if t == p else m_ref[at, :]
            c = []
            lacc = l_ref[at, :]
            for k in range(SUB):
                x = jnp.broadcast_to(rows[:, j0 + k:j0 + k + 1], (SUB, BLOCK))
                for m in range(k):
                    x = x - low[k, m] * c[m]
                c.append(x * inv[k])
                here = lane == j0 + k
                if t == p:
                    here = here & (sub >= k)
                lacc = jnp.where(here, c[k], lacc)
            l_ref[at, :] = lacc
            if t > p:
                x = jnp.where(inside, 0.0, rows)
                for k in range(SUB):
                    x = x - c[k] * u[k]
                m_ref[at, :] = x


def chol_kernel(coh_ref, sum_ref, out_ref, m_ref, l_ref, col_ref, row_ref, pan_ref):
    window = out_ref.shape[0]
    wide = sum_ref.shape[1]
    out_ref[...] = jnp.zeros_like(out_ref)
    at = 0
    for j in range(window // wide):
        size = window - j * wide
        out_ref[j * wide:, j * wide:(j + 1) * wide] = (
            coh_ref[j * wide:, j * wide:(j + 1) * wide] - sum_ref[at:at + size, :]
        )
        at += size

    row = lax.broadcasted_iota(jnp.int32, (window, BLOCK), 0)

    @pl.loop(0, window // BLOCK)
    def _(b):
        here = pl.ds(pl.multiple_of(b * BLOCK, BLOCK), BLOCK)
        pan_ref[...] = out_ref[:, here]

        @pl.loop(0, b)
        def _(k):
            there = pl.ds(pl.multiple_of(k * BLOCK, BLOCK), BLOCK)
            pan_ref[...] -= mul_nt(split(out_ref[:, there]), split(out_ref[here, there]))

        m_ref[...] = pan_ref[here, :]
        l_ref[...] = jnp.zeros_like(l_ref)
        factor_block(m_ref, l_ref, col_ref, row_ref)
        below = mul_nt(split(pan_ref[...]), split(m_ref[...]))
        out_ref[:, here] = jnp.where(row >= (b + 1) * BLOCK, below, 0.0)
        out_ref[here, here] = l_ref[...]


def cholesky(coh, packed):
    window = coh.shape[0]
    return pl.pallas_call(
        chol_kernel,
        name="factor",
        out_shape=jax.ShapeDtypeStruct((window, window), jnp.float32),
        in_specs=[pl.BlockSpec(memory_space=pltpu.VMEM)] * 2,
        out_specs=pl.BlockSpec(memory_space=pltpu.VMEM),
        scratch_shapes=[
            pltpu.VMEM((BLOCK, BLOCK), jnp.float32),
            pltpu.VMEM((BLOCK, BLOCK), jnp.float32),
            pltpu.VMEM((SUB, SUB, BLOCK), jnp.float32),
            pltpu.VMEM((SUB, BLOCK), jnp.float32),
            pltpu.VMEM((window, BLOCK), jnp.float32),
        ],
        compiler_params=pltpu.CompilerParams(vmem_limit_bytes=40 * 2**20),
        cost_estimate=pl.CostEstimate(flops=40 * 10**9, bytes_accessed=11 * 2**20, transcendentals=0),
    )(coh, packed)


cross_weight = 0.3


def coherence(spectra, nugget, decay):
    window = spectra.shape[0]
    col_ids = jnp.arange(window, dtype=jnp.int32)
    row_ids = col_ids
    row_global = PRIOR + row_ids
    col_global = PRIOR + col_ids
    row_points = row_global // 3
    col_points = col_global // 3
    row_across = (row_points % GRID).astype(jnp.float32)
    row_height = (row_points // GRID).astype(jnp.float32)
    col_across = (col_points % GRID).astype(jnp.float32)
    col_height = (col_points // GRID).astype(jnp.float32)
    distance = jnp.sqrt(
        (row_across[:, None] - col_across[None, :]) ** 2
        + (row_height[:, None] - col_height[None, :]) ** 2
    )
    coupling = jnp.where(
        (row_global % 3)[:, None] == (col_global % 3)[None, :],
        jnp.float32(1.0),
        jnp.float32(cross_weight),
    )
    amplitude = jnp.sqrt(spectra[:, None] * spectra[None, :])
    diagonal = jnp.where(
        row_ids[:, None] == col_ids[None, :], nugget[:, None], jnp.float32(0.0)
    )
    return coupling * amplitude * jnp.exp(-decay * distance) + diagonal


def against(picked, other):
    return lax.dot_general(
        picked, other, (((0,), (0,)), ((), ())), preferred_element_type=jnp.float32
    )


def waves_of(seeds):
    quarter = NPHASE // 4
    turn = (seeds + quarter // 2) // quarter
    x = (seeds - turn * quarter).astype(jnp.float32) * (2.0 * math.pi / NPHASE)
    y = x * x
    sin = x * (1.0 + y * (-1 / 6 + y * (1 / 120 + y * (-1 / 5040 + y * (1 / 362880)))))
    cos = 1.0 + y * (-1 / 2 + y * (1 / 24 + y * (-1 / 720 + y * (1 / 40320))))
    odd = (turn & 1) == 1
    re = jnp.where(odd, sin, cos)
    im = jnp.where(odd, cos, sin)
    return (
        jnp.where(((turn + 1) & 2) == 2, -re, re),
        jnp.where((turn & 2) == 2, -im, im),
    )


def synth_kernel(x_ref, table_ref, out_ref):
    def parts(value):
        high = value.astype(jnp.bfloat16).astype(jnp.float32)
        return high, value - high

    xh, xl = parts(x_ref[...])
    th, tl = parts(table_ref[...])
    lhs = jnp.concatenate([xh, xh, xl, xl], axis=0).astype(jnp.bfloat16)
    rhs = jnp.concatenate([th, tl, th, tl], axis=0).astype(jnp.bfloat16)
    out_ref[...] = lax.dot_general(
        lhs, rhs, (((0,), (0,)), ((), ())), preferred_element_type=jnp.float32
    )


def synthesize(stacked, freq_count):
    freq_bins = FIRST_BIN + jnp.arange(freq_count, dtype=jnp.int32)
    sample_ids = jnp.arange(STEPS, dtype=jnp.int32)
    turns = (freq_bins[:, None] * sample_ids[None, :] % STEPS).astype(jnp.float32) * (
        2.0 * math.pi / STEPS
    )
    tables = jnp.stack([jnp.cos(turns), -jnp.sin(turns)], axis=1).reshape(2 * freq_count, STEPS)
    count = stacked.shape[1]
    step = min(2048, count)
    return pl.pallas_call(
        synth_kernel,
        name="synth",
        grid=(count // step,),
        out_shape=jax.ShapeDtypeStruct((count, STEPS), jnp.float32),
        in_specs=[
            pl.BlockSpec((2 * freq_count, step), lambda i: (0, i)),
            pl.BlockSpec((2 * freq_count, STEPS), lambda i: (0, 0)),
        ],
        out_specs=pl.BlockSpec((step, STEPS), lambda i: (i, 0)),
        compiler_params=pltpu.CompilerParams(vmem_limit_bytes=24 * 2**20),
    )(stacked, tables)


def shards(prior_factor, prior_seeds, window_seeds, spectra, nugget, decay):
    cols = prior_factor[0]
    window = cols.shape[1]
    parts = lax.axis_size(AXES)
    freq_count = lax.axis_size("freq")
    quarter = window // (2 * parts)
    seed_count = prior_seeds.shape[2]
    me = lax.axis_index(AXES)
    wide = 2 * BLOCK

    packed = jnp.concatenate(
        [against(cols[:, at:], cols[:, at:at + wide]) for at in range(0, window, wide)], axis=0
    )
    packed = lax.psum_scatter(packed, AXES, scatter_dimension=0, tiled=True)

    def stored(wave):
        whole = against(cols, wave.astype(jnp.bfloat16)).reshape(2, parts, quarter, seed_count)
        return jnp.transpose(whole, (1, 0, 2, 3)).reshape(window, seed_count)

    wave_re, wave_im = waves_of(prior_seeds[0])
    whole = jnp.concatenate([stored(wave_re), stored(wave_im)], axis=1)
    coh = coherence(spectra[0], nugget[0], decay[0])
    window_waves = jnp.concatenate(waves_of(window_seeds[0]), axis=1)
    packed, whole = lax.optimization_barrier((packed, whole))
    packed = lax.all_gather(packed, AXES, axis=0, tiled=True)
    packed, whole, coh, window_waves = lax.optimization_barrier(
        (packed, whole, coh, window_waves)
    )
    prior = lax.psum_scatter(whole, AXES, scatter_dimension=0, tiled=True)

    factor = cholesky(coh, packed)
    own = jnp.concatenate(
        [
            lax.dynamic_slice_in_dim(factor, me * quarter, quarter, 0),
            lax.dynamic_slice_in_dim(factor, window // 2 + me * quarter, quarter, 0),
        ],
        axis=0,
    )
    amplitude = prior + jnp.dot(own, window_waves, precision=lax.Precision.HIGH)
    turned = amplitude.T.reshape(2, seed_count, 2 * quarter)
    spread = lax.all_to_all(turned, "freq", split_axis=1, concat_axis=0, tiled=True)
    here = seed_count // freq_count
    out = synthesize(spread.reshape(2 * freq_count, here * 2 * quarter), freq_count)
    return out.reshape(here, 2 * quarter, STEPS)


def solution(mesh):
    in_specs = (
        P("freq", ("row", "col"), None),
        P("freq", ("row", "col"), None),
        P("freq", None, None),
        P("freq", None),
        P("freq", None),
        P("freq"),
    )
    out_specs = P("freq", ("row", "col"), None)
    return jax.shard_map(shards, mesh=mesh, in_specs=in_specs, out_specs=out_specs, check_vma=False)
```

```python
import functools
import math

import jax
import jax.numpy as jnp
from jax import lax
from jax.experimental import pallas as pl
from jax.experimental.pallas import tpu as pltpu
from jax.sharding import PartitionSpec as P

GRID = 96
NPHASE = 4096
STEPS = 256
PRIOR = 26624
FIRST_BIN = 64
AXES = ("row", "col")
BLOCK = 128
SUB = 8


def split(x):
    high = x.astype(jnp.bfloat16)
    return high, (x - high.astype(jnp.float32)).astype(jnp.bfloat16)


def mul_nt(a, b):
    dims = (((1,), (1,)), ((), ()))
    dot = functools.partial(lax.dot_general, dimension_numbers=dims, preferred_element_type=jnp.float32)
    ah, al = a
    bh, bl = b
    return dot(ah, bh) + (dot(ah, bl) + dot(al, bh))


def factor_block(m_ref, l_ref, col_ref, row_ref):
    lane = lax.broadcasted_iota(jnp.int32, (SUB, BLOCK), 1)
    sub = lax.broadcasted_iota(jnp.int32, (SUB, BLOCK), 0)
    strips = BLOCK // SUB
    for p in range(strips):
        j0 = SUB * p
        inside = (lane >= j0) & (lane < j0 + SUB)
        lead = m_ref[j0:j0 + SUB, :]
        for k in range(SUB):
            col_ref[k] = jnp.broadcast_to(lead[:, j0 + k:j0 + k + 1], (SUB, BLOCK))
        row_ref[...] = jnp.where(inside, jnp.where(lane - j0 == sub, 1.0, 0.0), lead)
        a = {}
        for k in range(SUB):
            for i in range(k, SUB):
                a[i, k] = jnp.broadcast_to(col_ref[k, i:i + 1, :], (SUB, BLOCK))
        inv = []
        low = {}
        for k in range(SUB):
            r = lax.rsqrt(a[k, k])
            inv.append(r)
            for i in range(k + 1, SUB):
                low[i, k] = a[i, k] * r
            for m in range(k + 1, SUB):
                for i in range(m, SUB):
                    a[i, m] = a[i, m] - low[i, k] * low[m, k]
        u = []
        for k in range(SUB):
            x = jnp.broadcast_to(row_ref[k:k + 1, :], (SUB, BLOCK))
            for m in range(k):
                x = x - low[k, m] * u[m]
            u.append(x * inv[k])
        w = u[0]
        for k in range(1, SUB):
            w = jnp.where(sub == k, u[k], w)
        m_ref[j0:j0 + SUB, :] = jnp.where(lane < j0 + SUB, w, 0.0)
        for t in range(p, strips):
            at = slice(SUB * t, SUB * t + SUB)
            rows = lead if t == p else m_ref[at, :]
            c = []
            lacc = l_ref[at, :]
            for k in range(SUB):
                x = jnp.broadcast_to(rows[:, j0 + k:j0 + k + 1], (SUB, BLOCK))
                for m in range(k):
                    x = x - low[k, m] * c[m]
                c.append(x * inv[k])
                here = lane == j0 + k
                if t == p:
                    here = here & (sub >= k)
                lacc = jnp.where(here, c[k], lacc)
            l_ref[at, :] = lacc
            if t > p:
                x = jnp.where(inside, 0.0, rows)
                for k in range(SUB):
                    x = x - c[k] * u[k]
                m_ref[at, :] = x


def chol_kernel(coh_ref, sum_ref, out_ref, m_ref, l_ref, col_ref, row_ref, pan_ref):
    window = out_ref.shape[0]
    wide = sum_ref.shape[1]
    out_ref[...] = jnp.zeros_like(out_ref)
    at = 0
    for j in range(window // wide):
        size = window - j * wide
        out_ref[j * wide:, j * wide:(j + 1) * wide] = (
            coh_ref[j * wide:, j * wide:(j + 1) * wide] - sum_ref[at:at + size, :]
        )
        at += size

    row = lax.broadcasted_iota(jnp.int32, (window, BLOCK), 0)

    @pl.loop(0, window // BLOCK)
    def _(b):
        here = pl.ds(pl.multiple_of(b * BLOCK, BLOCK), BLOCK)
        pan_ref[...] = out_ref[:, here]

        @pl.loop(0, b)
        def _(k):
            there = pl.ds(pl.multiple_of(k * BLOCK, BLOCK), BLOCK)
            pan_ref[...] -= mul_nt(split(out_ref[:, there]), split(out_ref[here, there]))

        m_ref[...] = pan_ref[here, :]
        l_ref[...] = jnp.zeros_like(l_ref)
        factor_block(m_ref, l_ref, col_ref, row_ref)
        below = mul_nt(split(pan_ref[...]), split(m_ref[...]))
        out_ref[:, here] = jnp.where(row >= (b + 1) * BLOCK, below, 0.0)
        out_ref[here, here] = l_ref[...]


def cholesky(coh, packed):
    window = coh.shape[0]
    return pl.pallas_call(
        chol_kernel,
        name="factor",
        out_shape=jax.ShapeDtypeStruct((window, window), jnp.float32),
        in_specs=[pl.BlockSpec(memory_space=pltpu.VMEM)] * 2,
        out_specs=pl.BlockSpec(memory_space=pltpu.VMEM),
        scratch_shapes=[
            pltpu.VMEM((BLOCK, BLOCK), jnp.float32),
            pltpu.VMEM((BLOCK, BLOCK), jnp.float32),
            pltpu.VMEM((SUB, SUB, BLOCK), jnp.float32),
            pltpu.VMEM((SUB, BLOCK), jnp.float32),
            pltpu.VMEM((window, BLOCK), jnp.float32),
        ],
        compiler_params=pltpu.CompilerParams(vmem_limit_bytes=40 * 2**20),
        cost_estimate=pl.CostEstimate(flops=40 * 10**9, bytes_accessed=11 * 2**20, transcendentals=0),
    )(coh, packed)


cross_weight = 0.3


def coherence(spectra, nugget, decay):
    window = spectra.shape[0]
    col_ids = jnp.arange(window, dtype=jnp.int32)
    row_ids = col_ids
    row_global = PRIOR + row_ids
    col_global = PRIOR + col_ids
    row_points = row_global // 3
    col_points = col_global // 3
    row_across = (row_points % GRID).astype(jnp.float32)
    row_height = (row_points // GRID).astype(jnp.float32)
    col_across = (col_points % GRID).astype(jnp.float32)
    col_height = (col_points // GRID).astype(jnp.float32)
    distance = jnp.sqrt(
        (row_across[:, None] - col_across[None, :]) ** 2
        + (row_height[:, None] - col_height[None, :]) ** 2
    )
    coupling = jnp.where(
        (row_global % 3)[:, None] == (col_global % 3)[None, :],
        jnp.float32(1.0),
        jnp.float32(cross_weight),
    )
    amplitude = jnp.sqrt(spectra[:, None] * spectra[None, :])
    diagonal = jnp.where(
        row_ids[:, None] == col_ids[None, :], nugget[:, None], jnp.float32(0.0)
    )
    return coupling * amplitude * jnp.exp(-decay * distance) + diagonal


def against(picked, other):
    return lax.dot_general(
        picked, other, (((0,), (0,)), ((), ())), preferred_element_type=jnp.float32
    )


def waves_of(seeds):
    quarter = NPHASE // 4
    turn = (seeds + quarter // 2) // quarter
    x = (seeds - turn * quarter).astype(jnp.float32) * (2.0 * math.pi / NPHASE)
    y = x * x
    sin = x * (1.0 + y * (-1 / 6 + y * (1 / 120 + y * (-1 / 5040 + y * (1 / 362880)))))
    cos = 1.0 + y * (-1 / 2 + y * (1 / 24 + y * (-1 / 720 + y * (1 / 40320))))
    odd = (turn & 1) == 1
    re = jnp.where(odd, sin, cos)
    im = jnp.where(odd, cos, sin)
    return (
        jnp.where(((turn + 1) & 2) == 2, -re, re),
        jnp.where((turn & 2) == 2, -im, im),
    )


def quick_waves(seeds):
    quarter = NPHASE // 4
    turn = (seeds + quarter // 2) >> (quarter.bit_length() - 1)
    x = (seeds - turn * quarter).astype(jnp.float32) * (2.0 * math.pi / NPHASE)
    y = x * x
    sin = x * (1.0 + y * (-1 / 6 + y * (1 / 120 + y * (-1 / 5040 + y * (1 / 362880)))))
    cos = 1.0 + y * (-1 / 2 + y * (1 / 24 + y * (-1 / 720 + y * (1 / 40320))))
    odd = (turn & 1) == 1
    re = jnp.where(odd, sin, cos)
    im = jnp.where(odd, cos, sin)
    return (
        jnp.where(((turn + 1) & 2) == 2, -re, re),
        jnp.where((turn & 2) == 2, -im, im),
    )


def reduce_kernel(
    parts, n_col, packed_ref, cols_ref, seeds_ref, out_ref, prod_ref, sum_ref, land_ref, send_sem,
    recv_sem,
):
    me = lax.axis_index("row") * n_col + lax.axis_index("col")
    stages = parts.bit_length() - 1
    core = me % 2
    upper = [2**s for s in range(1, stages)]
    turned = upper[1:] + upper[:1]
    bits = [1] + [a + core * (b - a) for a, b in zip(upper, turned)]

    def partner(bit):
        other = me + bit * (1 - 2 * ((me // bit) % 2))
        return {"row": other // n_col, "col": other % n_col}

    barrier = pltpu.get_barrier_semaphore()
    for bit in bits:
        pl.semaphore_signal(
            barrier, inc=1, device_id=partner(bit), device_id_type=pl.DeviceIdType.MESH
        )
    pl.semaphore_wait(barrier, stages)

    depth, window = cols_ref.shape
    seed_count = seeds_ref.shape[1]
    own = prod_ref.shape[2]
    tall = 256
    chunk = next(c for c in (256, 208, 128, 64, 32, 16) if depth % c == 0)
    chunks = depth // chunk

    def products(first, last):
        @pl.loop(first, last)
        def _(step):
            at = pl.ds(pl.multiple_of(step * chunk, chunk), chunk)
            wave_re, wave_im = quick_waves(seeds_ref[at, :])
            waves = jnp.concatenate(
                [wave_re.astype(jnp.bfloat16), wave_im.astype(jnp.bfloat16)], axis=1
            )
            for r in range(window // tall):
                term = lax.dot_general(
                    cols_ref[at, r * tall:(r + 1) * tall],
                    waves,
                    (((0,), (0,)), ((), ())),
                    preferred_element_type=jnp.float32,
                ).reshape(tall // own, own, 2 * seed_count)
                half, base = divmod(r * tall, window // 2)
                there = slice(base // own, base // own + tall // own)
                prod_ref[there, half] += term

    share = [chunks * i // (2 * stages) for i in range(2 * stages + 1)]
    kept = []
    start, size, slot = 0, packed_ref.shape[0], 0
    for s, bit in enumerate(bits):
        size //= 2
        mine = (me // bit) % 2
        keep = pl.ds(pl.multiple_of(start + mine * size, 8), size)
        give = pl.ds(pl.multiple_of(start + (1 - mine) * size, 8), size)
        source = packed_ref if s == 0 else sum_ref
        landed = pl.ds(slot, size)
        copy = pltpu.make_async_remote_copy(
            src_ref=source.at[give],
            dst_ref=land_ref.at[landed],
            send_sem=send_sem.at[s],
            recv_sem=recv_sem.at[s],
            device_id=partner(bit),
            device_id_type=pl.DeviceIdType.MESH,
        )
        copy.start()
        if s == 0:
            prod_ref[...] = jnp.zeros_like(prod_ref)
        products(share[s], share[s + 1])
        copy.wait()
        total_ref = out_ref if s == stages - 1 else sum_ref
        total_ref[keep, :] = source[keep, :] + land_ref[landed, :]
        kept.append(keep)
        start = start + mine * size
        slot += size
    for back, s in enumerate(reversed(range(stages))):
        copy = pltpu.make_async_remote_copy(
            src_ref=out_ref.at[kept[s]],
            dst_ref=out_ref.at[kept[s]],
            send_sem=send_sem.at[stages + back],
            recv_sem=recv_sem.at[stages + back],
            device_id=partner(bits[s]),
            device_id_type=pl.DeviceIdType.MESH,
        )
        copy.start()
        products(share[stages + back], share[stages + back + 1])
        copy.wait()


def reduce_and_multiply(packed, cols, seeds, parts, n_col):
    window = cols.shape[1]
    quarter = window // (2 * parts)
    stages = parts.bit_length() - 1
    return pl.pallas_call(
        functools.partial(reduce_kernel, parts, n_col),
        name="reduce",
        out_shape=(
            jax.ShapeDtypeStruct(packed.shape, jnp.float32),
            jax.ShapeDtypeStruct((parts, 2, quarter, 2 * seeds.shape[1]), jnp.float32),
        ),
        in_specs=[pl.BlockSpec(memory_space=pltpu.VMEM)] * 3,
        out_specs=[pl.BlockSpec(memory_space=pltpu.VMEM)] * 2,
        scratch_shapes=[
            pltpu.VMEM(packed.shape, jnp.float32),
            pltpu.VMEM(packed.shape, jnp.float32),
            pltpu.SemaphoreType.DMA((2 * stages,)),
            pltpu.SemaphoreType.DMA((2 * stages,)),
        ],
        compiler_params=pltpu.CompilerParams(
            collective_id=0, has_side_effects=True, vmem_limit_bytes=48 * 2**20
        ),
    )(packed, cols, seeds)


def synth_kernel(x_ref, table_ref, out_ref):
    def parts(value):
        high = value.astype(jnp.bfloat16).astype(jnp.float32)
        return high, value - high

    xh, xl = parts(x_ref[...])
    th, tl = parts(table_ref[...])
    lhs = jnp.concatenate([xh, xh, xl, xl], axis=0).astype(jnp.bfloat16)
    rhs = jnp.concatenate([th, tl, th, tl], axis=0).astype(jnp.bfloat16)
    out_ref[...] = lax.dot_general(
        lhs, rhs, (((0,), (0,)), ((), ())), preferred_element_type=jnp.float32
    )


def synthesize(stacked, freq_count):
    freq_bins = FIRST_BIN + jnp.arange(freq_count, dtype=jnp.int32)
    sample_ids = jnp.arange(STEPS, dtype=jnp.int32)
    turns = (freq_bins[:, None] * sample_ids[None, :] % STEPS).astype(jnp.float32) * (
        2.0 * math.pi / STEPS
    )
    tables = jnp.stack([jnp.cos(turns), -jnp.sin(turns)], axis=1).reshape(2 * freq_count, STEPS)
    count = stacked.shape[1]
    step = min(2048, count)
    return pl.pallas_call(
        synth_kernel,
        name="synth",
        grid=(count // step,),
        out_shape=jax.ShapeDtypeStruct((count, STEPS), jnp.float32),
        in_specs=[
            pl.BlockSpec((2 * freq_count, step), lambda i: (0, i)),
            pl.BlockSpec((2 * freq_count, STEPS), lambda i: (0, 0)),
        ],
        out_specs=pl.BlockSpec((step, STEPS), lambda i: (i, 0)),
        compiler_params=pltpu.CompilerParams(vmem_limit_bytes=24 * 2**20),
    )(stacked, tables)


def shards(prior_factor, prior_seeds, window_seeds, spectra, nugget, decay):
    cols = prior_factor[0]
    window = cols.shape[1]
    parts = lax.axis_size(AXES)
    freq_count = lax.axis_size("freq")
    quarter = window // (2 * parts)
    seed_count = prior_seeds.shape[2]
    me = lax.axis_index(AXES)
    wide = 2 * BLOCK

    packed = jnp.concatenate(
        [against(cols[:, at:], cols[:, at:at + wide]) for at in range(0, window, wide)], axis=0
    )
    coh = coherence(spectra[0], nugget[0], decay[0])
    window_waves = jnp.concatenate(waves_of(window_seeds[0]), axis=1)
    packed, whole = reduce_and_multiply(packed, cols, prior_seeds[0], parts, lax.axis_size("col"))
    whole = whole.reshape(window, 2 * seed_count)
    prior = lax.psum_scatter(whole, AXES, scatter_dimension=0, tiled=True)

    factor = cholesky(coh, packed)
    own = jnp.concatenate(
        [
            lax.dynamic_slice_in_dim(factor, me * quarter, quarter, 0),
            lax.dynamic_slice_in_dim(factor, window // 2 + me * quarter, quarter, 0),
        ],
        axis=0,
    )
    amplitude = prior + jnp.dot(own, window_waves, precision=lax.Precision.HIGH)
    turned = amplitude.T.reshape(2, seed_count, 2 * quarter)
    spread = lax.all_to_all(turned, "freq", split_axis=1, concat_axis=0, tiled=True)
    here = seed_count // freq_count
    out = synthesize(spread.reshape(2 * freq_count, here * 2 * quarter), freq_count)
    return out.reshape(here, 2 * quarter, STEPS)


def solution(mesh):
    in_specs = (
        P("freq", ("row", "col"), None),
        P("freq", ("row", "col"), None),
        P("freq", None, None),
        P("freq", None),
        P("freq", None),
        P("freq"),
    )
    out_specs = P("freq", ("row", "col"), None)
    return jax.shard_map(shards, mesh=mesh, in_specs=in_specs, out_specs=out_specs, check_vma=False)
```
